32 devices in a mesh: wide: 8 (over z, y), narrow: 4 (over x, core).
Axes of the slice: x: 2, y: 2, z: 4, core: 2. Of those that a mesh axis runs over, the one named last changes fastest.
Arguments:
- coords_inner: float32 [2, 8192], P(None, ('wide', 'narrow')), may hold values from -1 to 1
- velocity: float32 [2, 8192], P(None, ('wide', 'narrow')), may hold values from -6 to 6
- source: float32 [8192], P(('wide', 'narrow')), may hold values from -6 to 6
- coords_edge: float32 [2, 4096], P(None, ('wide', 'narrow')), may hold values from -1 to 1
- flux_weight: float32 [2, 4096], P(None, ('wide', 'narrow')), may hold values from -6 to 6
- owner: int32 [4096, 1], P(('wide', 'narrow')), may hold values from 0 to 7; in each aligned block of 128 rows (0 to 127, 128 to 255, ...) at most 32 rows name the same one
- local_face: int32 [4096], P(('wide', 'narrow')), may hold values from 0 to 127
- w_first: float32 [2, 512], replicated, may hold values from -4 to 4
- b_first: float32 [512], replicated, may hold values from -3 to 3
- w_hidden: float32 [4, 512, 512], replicated, may hold values from -0.25 to 0.25
- b_hidden: float32 [4, 512], replicated, may hold values from -3 to 3
- w_last: float32 [512], replicated, may hold values from -0.25 to 0.25
Outputs:
- face_integral: float32 [1024], P('wide')
- grad_first: float32 [2, 512], replicated
- grad_hidden: float32 [4, 512, 512], replicated
- grad_last: float32 [512], replicated
The draws below stay inside these ranges and needn't reach their ends.
Inputs may be any that keep to these rules, and one draw needn't show every extreme that they name: Among the 128 face points of one device no owner appears more than 32 times, and some owner appears exactly 32 times.
All inputs are finite; a program needn't handle non-finite values.
Results may differ from the reference program's by a relative error of at most 0.0003.
Values sent between devices are 32-bit elements; how exact they have to be, the bound alone decides.
No kernel may reach another device: no remote copies, remote signals or barrier semaphores. Data moves between devices by JAX's collectives and lax.ppermute only.
A program may use at most 128 MiB of HBM per device.

```python
import math
import jax
import jax.numpy as jnp
import numpy as np
from jax import lax

D = 512
LAYERS = 4
PB = 128
FACE_DEV = 128
CAP = 32
NPI = 8192
NPB = 4096
NF = 1024
N_WIDE = 8
N_NARROW = 4


def draw_w_first(key, part):
    values = jax.random.uniform(jax.random.fold_in(key, 13), (2, D), jnp.float32, -4.0, 4.0)
    return values.astype(jnp.float32)


def draw_w_hidden(key, part):
    values = jnp.clip(0.15 * jax.random.normal(jax.random.fold_in(key, 22), (LAYERS, D, D), jnp.float32), -0.25, 0.25)
    return values.astype(jnp.float32)


def touch_ends(drawn, rng, smallest, high):
    longest = drawn.shape.index(max(drawn.shape))
    spots = []
    for shift in (0, 1):
        where = [jax.random.randint(jax.random.fold_in(rng, axis), (), 0, length) for axis, length in enumerate(drawn.shape)]
        where[longest] = (where[longest] + shift) % drawn.shape[longest]
        spots.append(tuple(where))
    return drawn.at[spots[0]].set(smallest).at[spots[1]].set(high)


def steps_of(rng, dims, shards, low, top_value):
    level = 1.0
    for dim, shards_of in shards:
        steps = jax.random.uniform(jax.random.fold_in(jax.random.fold_in(rng, 6), dim), (shards_of,), jnp.float32, low / len(shards), top_value / len(shards))
        level = level * jnp.repeat(jnp.exp(steps), dims[dim] // shards_of).reshape((-1,) + (1,) * (len(dims) - 1 - dim))
    return level


def assign_block(own_key, own, number, rows, number_of, top, reach, skew):
    ranking = jax.random.permutation(own_key, number_of)
    packed, common = load_shares(number_of, rows * top, reach, skew, True), load_shares(number_of, rows * top, reach, skew, False)
    places = jnp.arange(number_of)

    def named(tallies, offset_by):
        used = int((tallies > 0).sum())
        fixed = max(1, used // 4)
        passed = fixed + (places - fixed + offset_by * (used - fixed)) % max(1, number_of - fixed)
        return jnp.zeros((number_of,), jnp.int32).at[ranking[jnp.where(places < fixed, places, passed)]].set(jnp.asarray(tallies, jnp.int32))

    tallies = jnp.where(number % 4 == 0, named(packed, number // 4), named(common, number - number // 4 - 1))
    mixed = jax.random.permutation(jax.random.fold_in(own, 3), number_of)
    source_of, receiver = mixed[0:number_of // 2 * 2:2], mixed[1:number_of // 2 * 2:2]
    margin = jnp.minimum(tallies[source_of] - 1, reach - tallies[receiver]) // 2
    margin = jnp.where((source_of == ranking[0]) | (receiver == ranking[0]) | (tallies[receiver] == 0), 0, jnp.maximum(margin, 0))
    passed = jax.random.randint(jax.random.fold_in(own, 4), (number_of // 2,), 0, 1 << 20) % (margin + 1)
    tallies = tallies.at[source_of].add(-passed).at[receiver].add(passed)
    labels = jnp.searchsorted(jnp.cumsum(tallies), jnp.arange(rows * top), side="right").astype(jnp.int32)
    listing = labels.reshape(top, rows).T
    listing = listing[jax.random.permutation(jax.random.fold_in(own, 1), rows)]
    offset_by = jax.random.randint(jax.random.fold_in(own, 2), (rows, 1), 0, top)
    return jnp.take_along_axis(listing, (jnp.arange(top)[None, :] + offset_by) % top, axis=1)


def load_shares(count, total, limit, skew, full):
    loads = [(1 << 20) // math.isqrt(standing ** skew) + 1 for standing in range(1, count + 1)]
    largest = limit if full else min(limit, max(-(-total // count), total * loads[0] // sum(loads)))
    least = 1 if total - largest >= count - 1 else 0
    given, surplus = [largest] + [least] * (count - 1), total - largest - least * (count - 1)
    while surplus > 0:
        candidates = [i for i in range(1, count) if given[i] < largest] or [i for i in range(1, count) if given[i] < limit]
        mass, left = sum([loads[i] for i in candidates]), surplus
        for i in candidates:
            more = min(limit - given[i], max(1, left * loads[i] // mass), surplus)
            given[i] = given[i] + more
            surplus = surplus - more
    return np.array(given)


def scatter_about(stream_key, extent, scale, most, cuts=(), held_as=jnp.bfloat16):
    entries = jax.random.normal(stream_key, extent, jnp.float32) * scale
    if len(cuts) > 0:
        entries = steps_of(stream_key, extent, cuts, -0.22, 0.18) * entries
    return jnp.clip(entries, min=-most, max=most).astype(held_as)


def setup_inputs(seed: int = 0) -> dict:
    key_of = jax.random.split(jax.random.key(seed), 13)
    coords_inner = jnp.clip(jax.random.uniform(key_of[0], (2, NPI), jnp.float32, -1.0, 1.0) * steps_of(key_of[0], (2, NPI), ((1, 32),), -0.4, 0.0), -1.0, 1.0)
    velocity = scatter_about(key_of[1], (2, NPI), 1.0, 6.0, ((1, 32),), jnp.float32)
    source = scatter_about(key_of[2], (NPI,), 1.0, 6.0, ((0, 32),), jnp.float32)
    coords_edge = jnp.clip(jax.random.uniform(key_of[3], (2, NPB), jnp.float32, -1.0, 1.0) * steps_of(key_of[3], (2, NPB), ((1, 32),), -0.4, 0.0), -1.0, 1.0)
    flux_weight = scatter_about(key_of[4], (2, NPB), 1.0, 6.0, ((1, 32),), jnp.float32)
    owner_keys = jax.random.split(jax.random.fold_in(key_of[5], 1), NPB // PB)
    owner_turns = jax.random.permutation(jax.random.fold_in(key_of[5], 3), NPB // PB)
    owner = jax.vmap(lambda own, number: assign_block(jax.random.fold_in(key_of[5], 2), own, number, PB, N_WIDE, 1, CAP, 2))(owner_keys, owner_turns).reshape((NPB, 1))
    local_face = touch_ends(jax.random.randint(key_of[6], (NPB,), 0, FACE_DEV), jax.random.fold_in(key_of[6], 1), 0, FACE_DEV - 1).astype(jnp.int32)
    w_first = draw_w_first(jax.random.fold_in(key_of[12], 71), 0)
    b_first = scatter_about(key_of[8], (D,), 0.5, 3.0, (), jnp.float32)
    w_hidden = draw_w_hidden(jax.random.fold_in(key_of[12], 71), 0)
    b_hidden = scatter_about(key_of[10], (LAYERS, D), 0.5, 3.0, (), jnp.float32)
    w_last = scatter_about(key_of[11], (D,), D ** -0.5, 0.25, (), jnp.float32)
    return {"coords_inner": coords_inner, "velocity": velocity, "source": source, "coords_edge": coords_edge, "flux_weight": flux_weight, "owner": owner, "local_face": local_face, "w_first": w_first, "b_first": b_first, "w_hidden": w_hidden, "b_hidden": b_hidden, "w_last": w_last}


precise = lax.Precision.HIGHEST
penalty_weight = 4.0

def network(weights, biases, coords):
    w_first, w_hidden, w_last = weights
    b_first, b_hidden = biases
    point_count = coords.shape[1]
    feature_width = w_first.shape[1]
    hidden = jnp.tanh(jnp.dot(coords.T, w_first, precision=precise) + b_first)
    tangent = (1.0 - hidden * hidden)[None] * w_first[:, None, :]
    for level_index in range(w_hidden.shape[0]):
        stacked = jnp.concatenate([hidden[None], tangent], 0).reshape(3 * point_count, feature_width)
        product = jnp.dot(stacked, w_hidden[level_index], precision=precise)
        hidden = jnp.tanh(product[:point_count] + b_hidden[level_index])
        tangent = (1.0 - hidden * hidden)[None] * product[point_count:].reshape(2, point_count, feature_width)
    point_value = jnp.dot(hidden, w_last, precision=precise)
    slopes = jnp.dot(tangent.reshape(2 * point_count, feature_width), w_last, precision=precise).reshape(2, point_count)
    return (point_value, slopes)

def residual(weights, biases, coords, velocity, source):
    point_value, slopes = network(weights, biases, coords)
    return velocity[0] * slopes[0] + velocity[1] * slopes[1] + point_value - source

def edge_flux(weights, biases, coords, flux_weight):
    _, slopes = network(weights, biases, coords)
    return flux_weight[0] * slopes[0] + flux_weight[1] * slopes[1]

def reference(coords_inner, velocity, source, coords_edge, flux_weight, owner, local_face, w_first, b_first, w_hidden, b_hidden, w_last):
    weights = (w_first, w_hidden, w_last)
    biases = (b_first, b_hidden)
    blocks = N_WIDE * N_NARROW

    def split(array):
        shaped = array.reshape(array.shape[:-1] + (blocks, array.shape[-1] // blocks))
        return jnp.moveaxis(shaped, -2, 0)
    edge_coords = split(coords_edge)
    edge_weight = split(flux_weight)
    fluxes = lax.map(lambda pair: edge_flux(weights, biases, pair[0], pair[1]), (edge_coords, edge_weight)).reshape(-1)
    face_index = owner[:, 0] * FACE_DEV + local_face
    integral = jax.ops.segment_sum(fluxes, face_index, num_segments=NF)
    edge_cot = split(2.0 * penalty_weight / math.sqrt(NF) * integral[face_index])

    def accumulate(totals, pieces):
        inner_c, inner_v, inner_s, edge_c, edge_w, cotangent = pieces
        residuals, inner_pull = jax.vjp(lambda params: residual(params, biases, inner_c, inner_v, inner_s), weights)
        inner_grads = inner_pull(2.0 / math.sqrt(NPI) * residuals)[0]
        _, edge_pull = jax.vjp(lambda params: edge_flux(params, biases, edge_c, edge_w), weights)
        edge_grads = edge_pull(cotangent)[0]
        return (jax.tree.map(lambda first, second, third: first + second + third, totals, inner_grads, edge_grads), None)
    start = (jnp.zeros_like(w_first), jnp.zeros_like(w_hidden), jnp.zeros_like(w_last))
    totals, _ = lax.scan(accumulate, start, (split(coords_inner), split(velocity), split(source), edge_coords, edge_weight, edge_cot))
    return (integral, totals[0], totals[1], totals[2])
```

```python
import functools
import math

import jax
import jax.numpy as jnp
from jax import lax
from jax.experimental import pallas as pl
from jax.experimental.pallas import tpu as pltpu
from jax.sharding import PartitionSpec as P

FACE_DEV = 128
LANES = 128
SUB = 8
AXES = ("wide", "narrow")
F32, BF16 = jnp.float32, jnp.bfloat16
exact = lax.Precision.HIGHEST
penalty_weight = 4.0
NN = (((1,), (0,)), ((), ()))
NT = (((1,), (1,)), ((), ()))


def split(x):
    high = x.astype(BF16)
    return high, (x - high.astype(F32)).astype(BF16)


def dot(a, b, dims=NN):
    return lax.dot_general(a, b, dims, preferred_element_type=F32)


def dot3(a, b, dims=NN):
    return dot(a[0], b[0], dims) + (dot(a[0], b[1], dims) + dot(a[1], b[0], dims))


def column(row, count):
    turned = jnp.broadcast_to(row, (LANES, row.shape[1])).T
    return jnp.concatenate([turned] * (count // LANES), 1)


def stacked(hidden, slopes):
    n = hidden.shape[1]
    scale = 1.0 - hidden * hidden
    return split(hidden), split(scale * slopes[:, :n]), split(scale * slopes[:, n:])


def join(parts):
    return tuple(jnp.concatenate([p[i] for p in parts], 1) for i in (0, 1))


def spec(block, index=None):
    return pl.BlockSpec(block, index or (lambda i: (0,) * len(block)))


def forward_kernel(first, last, n, d, *refs):
    refs = list(refs)
    take = lambda k: [refs.pop(0) for _ in range(k)]
    (weight,) = take(1)
    (bias,) = take(1)
    start = take(3) if first else take(2)
    tail = take(1) if last else []
    hs, ps, h_end, p_end = take(4)
    sums = take(1) if last else []
    h, p = take(2)
    step = pl.program_id(0)

    @pl.when(step == 0)
    def _():
        if first:
            coords, w_first, b_first = start
            a, b = column(w_first[0:1, :], n), column(w_first[1:2, :], n)
            pre = a * coords[0:1, :] + b * coords[1:2, :] + column(b_first[...], n)
            h[...] = jnp.tanh(pre)
            p[:, :n] = a
            p[:, n:] = b
        else:
            h[...] = start[0][...]
            p[...] = start[1][...]

    hidden, slopes = h[...], p[...]
    hs[0] = hidden
    ps[0] = slopes
    x = join(stacked(hidden, slopes))
    product = dot3(split(weight[0].T), x)
    new = jnp.tanh(product[:, :n] + column(bias[0], n))
    h[...] = new
    p[...] = product[:, n:]

    @pl.when(step == pl.num_programs(0) - 1)
    def _():
        new, slopes = h[...], p[...]
        h_end[...] = new
        p_end[...] = slopes
        if last:
            row = jnp.broadcast_to(tail[0][...], (SUB, d))
            sums[0][...] = dot3(split(row), join(stacked(new, slopes)))


def forward(n, d, k0, nl, w_hidden, b_hidden, start, w_last):
    first, last = len(start) == 3, w_last is not None
    in_specs = [spec((1, d, d), lambda i: (k0 + i, 0, 0)), spec((1, 1, d), lambda i: (k0 + i, 0, 0))]
    in_specs += [spec(a.shape) for a in start]
    args = [w_hidden, b_hidden, *start]
    out_shape = [(nl, d, n), (nl, d, 2 * n), (d, n), (d, 2 * n)]
    out_specs = [
        spec((1, d, n), lambda i: (i, 0, 0)),
        spec((1, d, 2 * n), lambda i: (i, 0, 0)),
        spec((d, n)),
        spec((d, 2 * n)),
    ]
    if last:
        in_specs.append(spec((1, d)))
        args.append(w_last)
        out_shape.append((SUB, 3 * n))
        out_specs.append(spec((SUB, 3 * n)))
    return pl.pallas_call(
        functools.partial(forward_kernel, first, last, n, d),
        grid=(nl,),
        in_specs=in_specs,
        out_specs=out_specs,
        out_shape=[jax.ShapeDtypeStruct(s, F32) for s in out_shape],
        scratch_shapes=[pltpu.VMEM((d, n), F32), pltpu.VMEM((d, 2 * n), F32)],
        cost_estimate=pl.CostEstimate(
            flops=18 * nl * d * d * n, bytes_accessed=4 * nl * d * (d + 3 * n), transcendentals=nl * d * n
        ),
        name="forward",
    )(*args)


def place_kernel(sums, flux_weight, owner, face, out, owners):
    n = flux_weight.shape[1]
    row = sums[0:1, :]
    flux = flux_weight[0:1, :] * row[:, n : 2 * n] + flux_weight[1:2, :] * row[:, 2 * n :]
    hot = (owner[...] == lax.broadcasted_iota(jnp.int32, (n, LANES), 1)).astype(F32).T
    hot = hot[: out.shape[0]]
    owners[...] = hot
    faces = (face[...] == lax.broadcasted_iota(jnp.int32, (FACE_DEV, n), 0)).astype(F32)
    out[...] = lax.dot_general(hot * flux, faces, NT, precision=exact, preferred_element_type=F32)


def place(wide, sums, flux_weight, owner, face):
    n = flux_weight.shape[1]
    return pl.pallas_call(
        place_kernel,
        out_shape=[jax.ShapeDtypeStruct((wide, FACE_DEV), F32), jax.ShapeDtypeStruct((wide, n), F32)],
        name="place",
    )(sums, flux_weight, owner, face)


def owner_of(me, own, other, position):
    a, b = own[position], other[position]
    if a == b:
        return me ^ a
    return me ^ jnp.where(me % 2 == 0, a, b)


def scatter(me, tables, per, flat, keep, send, extra=0):
    count = len(tables[0])
    half = count // 2
    for position in range(count):
        target, place_at = (keep, position) if position < half else (send, position - half)
        first = owner_of(me, *tables, position) * SUB
        for unit in range(per):
            start = pl.multiple_of(first + unit * SUB * count, SUB)
            target[place_at, unit * SUB : (unit + 1) * SUB, :] = flat[pl.ds(start, SUB), :]


def differentials(hidden, slopes, cot):
    n = hidden.shape[1]
    scale = 1.0 - hidden * hidden
    d_hidden, d_0, d_1 = cot[:, :n], cot[:, n : 2 * n], cot[:, 2 * n :]
    d_scale = d_0 * slopes[:, :n] + d_1 * slopes[:, n:]
    return scale * (d_hidden - 2.0 * hidden * d_scale), scale * d_0, scale * d_1


def backward_kernel(opening, closing, ni, ne, d, tables, face_scale, inner_scale, per, *refs):
    refs = list(refs)
    take = lambda k: [refs.pop(0) for _ in range(k)]
    (where,) = take(1)
    (weight,) = take(1)
    lower = take(4)
    upper = take(4)
    if opening:
        isums, velocity, source, full, owners, face, flux_weight, w_last = take(8)
    else:
        cot_in = take(2)
        (g_last,) = take(1)
    if closing:
        coords = take(2)
    keep, send = take(2)
    if opening:
        cot_out = take(2)
        (g_last,) = take(1)
    if closing:
        keep_more, send_more = take(2)
    top = take(4)
    cots = take(2)
    xh, xl, dh, dl, flat = take(5)
    step = pl.program_id(0)
    me = where[0]
    sizes, offsets = (ni, ne), (0, 3 * ni)

    @pl.when(step == 0)
    def _():
        for a, b in zip(top, upper):
            a[...] = b[...]
        if not opening:
            for a, b in zip(cots, cot_in):
                a[...] = b[...]
            return
        row = isums[0:1, :]
        res = velocity[0:1, :] * row[:, ni : 2 * ni] + velocity[1:2, :] * row[:, 2 * ni :]
        res = inner_scale * (res + row[:, :ni] - source[...])
        inner = (res, res * velocity[0:1, :], res * velocity[1:2, :])
        faces = (face[...] == lax.broadcasted_iota(jnp.int32, (FACE_DEV, ne), 0)).astype(F32)
        found = lax.dot_general(full[...], faces, NN, precision=exact, preferred_element_type=F32)
        found = face_scale * jnp.sum(owners[...] * found, 0, keepdims=True)
        edge = (jnp.zeros_like(found), found * flux_weight[0:1, :], found * flux_weight[1:2, :])
        total = None
        for group, rows in enumerate((inner, edge)):
            n = sizes[group]
            line = jnp.concatenate(rows, 1)
            lift = column(w_last[...], LANES)
            for tile in range(3 * n // LANES):
                at = slice(tile * LANES, (tile + 1) * LANES)
                cots[group][:, at] = lift * line[:, at]
            x = join(stacked(top[2 * group][...], top[2 * group + 1][...]))
            part = dot3(split(jnp.broadcast_to(line, (SUB, 3 * n))), x, NT)
            total = part if total is None else total + part
        g_last[...] = total

    for group in (0, 1):
        n, at = sizes[group], offsets[group]
        parts = differentials(top[2 * group][...], top[2 * group + 1][...], cots[group][...])
        for j, part in enumerate(parts):
            high, low = split(part)
            dh[:, at + j * n : at + (j + 1) * n] = high
            dl[:, at + j * n : at + (j + 1) * n] = low
        hidden, slopes = lower[2 * group][0], lower[2 * group + 1][0]
        for j, (high, low) in enumerate(stacked(hidden, slopes)):
            xh[:, at + j * n : at + (j + 1) * n] = high
            xl[:, at + j * n : at + (j + 1) * n] = low
        top[2 * group][...] = hidden
        top[2 * group + 1][...] = slopes

    x, delta = (xh[...], xl[...]), (dh[...], dl[...])
    grad = dot3(x, delta, NT)
    for tile in range(d // LANES):
        flat[tile * d : (tile + 1) * d, :] = grad[:, tile * LANES : (tile + 1) * LANES]
    back = dot3(split(weight[0]), delta)
    cots[0][...] = back[:, : 3 * ni]
    cots[1][...] = back[:, 3 * ni :]
    scatter(me, tables, per, flat, keep, send)

    @pl.when(step == pl.num_programs(0) - 1)
    def _():
        if opening:
            for a, b in zip(cot_out, cots):
                a[...] = b[...]
        if closing:
            total = None
            for group in (0, 1):
                n = sizes[group]
                delta = join([split(p) for p in differentials(top[2 * group][...], top[2 * group + 1][...], cots[group][...])])
                one, none = jnp.ones((1, n), F32), jnp.zeros((1, n), F32)
                c = coords[group]
                rows = jnp.concatenate(
                    [
                        jnp.concatenate([c[0:1, :], one, none], 1),
                        jnp.concatenate([c[1:2, :], none, one], 1),
                        jnp.zeros((SUB - 2, 3 * n), F32),
                    ],
                    0,
                )
                part = dot3(split(rows), delta, NT)
                total = part if total is None else total + part
            line = lambda row: [row[:, t * LANES : (t + 1) * LANES] for t in range(d // LANES)]
            rows = line(g_last[0:1, :]) + line(total[0:1, :]) + line(total[1:2, :])
            while len(rows) % SUB:
                rows.append(jnp.zeros((1, LANES), F32))
            pages = [jnp.concatenate(rows[i : i + SUB], 0) for i in range(0, len(rows), SUB)]
            half = len(tables[0]) // 2
            for position in range(2 * half):
                owner = owner_of(me, *tables, position)
                value = jnp.zeros((SUB, LANES), F32)
                for i, page in enumerate(pages):
                    value = jnp.where(owner == i, page, value)
                if position < half:
                    keep_more[position] = value
                else:
                    send_more[position - half] = value


def backward(me, k0, nl, w_hidden, lower, upper, opened, carried, coords, tables, scales):
    opening, closing = opened is not None, coords is not None
    d = w_hidden.shape[1]
    stacks, bases = zip(*lower)
    ni, ne = stacks[0].shape[2], stacks[2].shape[2]
    count = len(tables[0])
    per = d * d // LANES // (SUB * count)
    half = count // 2
    args, in_specs = [me, w_hidden], [
        pl.BlockSpec(memory_space=pltpu.SMEM),
        spec((1, d, d), lambda i: (k0 + nl - 1 - i, 0, 0)),
    ]
    for stack, base in lower:
        args.append(stack)
        in_specs.append(spec((1,) + stack.shape[1:], lambda i, base=base: (base + nl - 1 - i, 0, 0)))
    for array, level in upper:
        args.append(array)
        if level is None:
            in_specs.append(spec(array.shape))
        else:
            in_specs.append(pl.BlockSpec((pl.Squeezed(),) + array.shape[1:], lambda i, level=level: (level, 0, 0)))
    for array in opened if opening else carried:
        args.append(array)
        in_specs.append(spec(array.shape))
    for array in coords or ():
        args.append(array)
        in_specs.append(spec(array.shape))
    out_shape = [(half, nl * per * SUB, LANES)] * 2
    out_specs = [spec((half, per * SUB, LANES), lambda i: (0, i, 0))] * 2
    more = []
    if opening:
        more += [(d, 3 * ni), (d, 3 * ne), (SUB, d)]
    if closing:
        more += [(half, SUB, LANES)] * 2
    out_shape += more
    out_specs += [spec(s) for s in more]
    points = ni + ne
    return pl.pallas_call(
        functools.partial(backward_kernel, opening, closing, ni, ne, d, tables, *scales, per),
        grid=(nl,),
        in_specs=in_specs,
        out_specs=out_specs,
        out_shape=[jax.ShapeDtypeStruct(s, F32) for s in out_shape],
        scratch_shapes=[
            pltpu.VMEM((d, ni), F32),
            pltpu.VMEM((d, 2 * ni), F32),
            pltpu.VMEM((d, ne), F32),
            pltpu.VMEM((d, 2 * ne), F32),
            pltpu.VMEM((d, 3 * ni), F32),
            pltpu.VMEM((d, 3 * ne), F32),
        ]
        + [pltpu.VMEM((d, 3 * points), BF16)] * 4
        + [pltpu.VMEM((d * d // LANES, LANES), F32)],
        cost_estimate=pl.CostEstimate(
            flops=36 * nl * d * d * points, bytes_accessed=4 * nl * d * (2 * d + 3 * points), transcendentals=0
        ),
        name="backward",
    )(*args)


def hop(array, pairs):
    return lax.ppermute(array, AXES, pairs)


def orders_of(count, turn):
    bits = [1 << i for i in range(1, count.bit_length() - 1)]
    bits = bits[turn:] + bits[:turn]
    swapped = list(bits)
    for i in range(0, len(bits) - 1, 2):
        swapped[i], swapped[i + 1] = bits[i + 1], bits[i]
    return bits, swapped


def tables_of(count, orders):
    def offsets(order):
        found = [0]
        for bit in reversed(order):
            found = found + [bit ^ f for f in found]
        return found

    even, odd = offsets(orders[0]), offsets(orders[1])
    return tuple(even + [1 ^ f for f in odd]), tuple(odd + [1 ^ f for f in even])


def pairs_of(count, orders, stage):
    if stage == 0:
        return [(i, i ^ 1) for i in range(count)]
    return [(i, i ^ orders[i % 2][stage - 1]) for i in range(count)]


def total(count, orders, keep, send):
    stages = count.bit_length() - 1
    for stage in range(stages - 1):
        held = keep + hop(send, pairs_of(count, orders, stage))
        if stage < stages - 2:
            middle = held.shape[0] // 2
            keep, send = held[:middle], held[middle:]
    came = hop(held, pairs_of(count, orders, stages - 1))
    held = held + jnp.concatenate([came[1:], came[:1]], 0)
    for stage in range(stages - 2, 0, -1):
        held = jnp.concatenate([held, hop(held, pairs_of(count, orders, stage))], 0)
    return held, hop(held, pairs_of(count, orders, 0))


def gather_kernel(tables, steps, per, d, *refs):
    where, *halves = refs[:-1]
    out = refs[-1]
    me = where[0]
    count = len(tables[0][0])
    rows = SUB * count
    for chunk, layers in enumerate(steps):

        @pl.when(functools.reduce(jnp.logical_or, [pl.program_id(0) == s for s in layers]))
        def _(chunk=chunk):
            for position in range(count):
                source = halves[2 * chunk + position // (count // 2)]
                first = owner_of(me, *tables[chunk], position) * SUB
                for unit in range(per):
                    value = source[position % (count // 2), unit * SUB : (unit + 1) * SUB, :]
                    if rows <= d:
                        tile = unit * rows // d
                        start = pl.multiple_of(first + unit * rows % d, SUB)
                        out[0, pl.ds(start, SUB), tile * LANES : (tile + 1) * LANES] = value
                    else:
                        flat = first + unit * rows
                        start = pl.multiple_of(flat % d, SUB)
                        tile = pl.multiple_of(flat // d * LANES, LANES)
                        out[0, pl.ds(start, SUB), pl.ds(tile, LANES)] = value


def gather(me, d, tables, steps, parts):
    count = len(tables[0][0])
    per = d * d // LANES // (SUB * count)
    order = [layer for layers in steps for layer in layers]
    layer_count = len(order)
    place = [order.index(i) for i in range(layer_count)]
    half = count // 2
    in_specs = [pl.BlockSpec(memory_space=pltpu.SMEM)]
    base = 0
    where = []
    for layers in steps:
        nl = len(layers)
        in_specs += [spec((half, per * SUB, LANES), lambda i, b=base, n=nl: (0, jnp.clip(i - b, 0, n - 1), 0))] * 2
        where.append(tuple(range(base, base + nl)))
        base += nl

    def layer_at(i):
        value = order[0]
        for s, layer in enumerate(order[1:]):
            value = jnp.where(i == s + 1, layer, value)
        return value

    return pl.pallas_call(
        functools.partial(gather_kernel, tables, where, per, d),
        grid=(layer_count,),
        in_specs=in_specs,
        out_specs=spec((1, d, d), lambda i: (layer_at(i), 0, 0)),
        out_shape=jax.ShapeDtypeStruct((layer_count, d, d), F32),
        name="gather",
    )(me, *parts)


def local(
    coords_inner,
    velocity,
    source,
    coords_edge,
    flux_weight,
    owner,
    local_face,
    w_first,
    b_first,
    w_hidden,
    b_hidden,
    w_last,
):
    wide, narrow = lax.axis_size("wide"), lax.axis_size("narrow")
    count = wide * narrow
    layers, d = w_hidden.shape[:2]
    ni, ne = coords_inner.shape[1], coords_edge.shape[1]
    inner_scale = 2.0 / math.sqrt(ni * count)
    face_scale = 2.0 * penalty_weight / math.sqrt(FACE_DEV * wide)
    index = lax.axis_index("wide") * narrow + lax.axis_index("narrow")
    me = index.astype(jnp.int32)[None]
    face = local_face[None]
    b_hidden = b_hidden[:, None]
    b_first, w_last, source = b_first[None], w_last[None], source[None]
    middle = layers // 2

    eh, ep, eh_end, ep_end, esums = forward(
        ne, d, 0, layers, w_hidden, b_hidden, (coords_edge, w_first, b_first), w_last
    )
    full, owners = place(wide, esums, flux_weight, owner, face)
    for bit in range(count.bit_length() - 1):
        full = full + hop(full, [(i, i ^ (1 << bit)) for i in range(count)])
    ih0, ip0, ih_mid, ip_mid = forward(
        ni, d, 0, middle, w_hidden, b_hidden, (coords_inner, w_first, b_first), None
    )
    ih1, ip1, ih_end, ip_end, isums = forward(
        ni, d, middle, layers - middle, w_hidden, b_hidden, (ih_mid, ip_mid), w_last
    )

    orders = (orders_of(count, 0), orders_of(count, 2))
    tables = tuple(tables_of(count, o) for o in orders)
    scales = (face_scale, inner_scale)
    keep_a, send_a, cot_i, cot_e, g_last = backward(
        me,
        middle,
        layers - middle,
        w_hidden,
        ((ih1, 0), (ip1, 0), (eh, middle), (ep, middle)),
        ((ih_end, None), (ip_end, None), (eh_end, None), (ep_end, None)),
        (isums, velocity, source, full, owners, face, flux_weight, w_last),
        None,
        None,
        tables[0],
        scales,
    )
    keep_b, send_b, keep_x, send_x = backward(
        me,
        0,
        middle,
        w_hidden,
        ((ih0, 0), (ip0, 0), (eh, 0), (ep, 0)),
        ((ih_mid, None), (ip_mid, None), (eh, middle), (ep, middle)),
        None,
        (cot_i, cot_e, g_last),
        (coords_inner, coords_edge),
        tables[1],
        scales,
    )
    keep_b, send_b = jnp.concatenate([keep_b, keep_x], 1), jnp.concatenate([send_b, send_x], 1)
    own_a, other_a = total(count, orders[0], keep_a, send_a)
    own_b, other_b = total(count, orders[1], keep_b, send_b)
    steps = (tuple(range(layers - 1, middle - 1, -1)), tuple(range(middle - 1, -1, -1)))
    grad_hidden = gather(me, d, tables, steps, (own_a, other_a, own_b, other_b))

    pages = []
    per_page = SUB * LANES
    both = jnp.concatenate([own_b[:, -SUB:], other_b[:, -SUB:]], 0)
    table = jnp.where(index % 2 == 0, jnp.array(tables[1][0]), jnp.array(tables[1][1])) ^ index
    for page in range(-(-3 * d // per_page)):
        pages.append(jnp.sum(jnp.where((table == page)[:, None, None], both, 0.0), 0).reshape(-1))
    small = jnp.concatenate(pages)
    integral = lax.dynamic_index_in_dim(full, lax.axis_index("wide"), 0, keepdims=False)
    return (integral, small[d : 3 * d].reshape(2, d), grad_hidden, small[:d])


def solution(mesh):
    placed = (
        P(None, AXES),
        P(None, AXES),
        P(AXES),
        P(None, AXES),
        P(None, AXES),
        P(AXES, None),
        P(AXES),
        P(),
        P(),
        P(),
        P(),
        P(),
    )
    return jax.shard_map(
        local, mesh=mesh, in_specs=placed, out_specs=(P("wide"), P(), P(), P()), check_vma=False
    )
```

```python
import functools
import math

import jax
import jax.numpy as jnp
from jax import lax
from jax.experimental import pallas as pl
from jax.experimental.pallas import tpu as pltpu
from jax.sharding import PartitionSpec as P


FACE_DEV = 128
LANES = 128
SUB = 8
AXES = ("wide", "narrow")
ROOM = {"edge": 8, "inner": 3, "backward": 11, "gather": 4}


def CHUNKS(layers):
    middle = layers // 2
    return (
        (tuple(range(layers - 1, middle - 1, -1)), (0, 1)),
        (tuple(range(middle - 1, -1, -1)), (2, 0)),
    )


F32, BF16 = jnp.float32, jnp.bfloat16
exact = lax.Precision.HIGHEST
penalty_weight = 4.0
NN = (((1,), (0,)), ((), ()))
NT = (((1,), (1,)), ((), ()))


def split(x):
    high = x.astype(BF16)
    return high, (x - high.astype(F32)).astype(BF16)


def dot(a, b, dims=NN):
    return lax.dot_general(a, b, dims, preferred_element_type=F32)


def dot3(a, b, dims=NN):
    return dot(a[0], b[0], dims) + (dot(a[0], b[1], dims) + dot(a[1], b[0], dims))


def column(row, count):
    turned = jnp.broadcast_to(row, (LANES, row.shape[1])).T
    return jnp.concatenate([turned] * (count // LANES), 1)


def stacked(hidden, slopes):
    n = hidden.shape[1]
    scale = 1.0 - hidden * hidden
    return split(hidden), split(scale * slopes[:, :n]), split(scale * slopes[:, n:])


def join(parts):
    return tuple(jnp.concatenate([p[i] for p in parts], 1) for i in (0, 1))


VMEM = pl.BlockSpec(memory_space=pltpu.VMEM)
SMEM = pl.BlockSpec(memory_space=pltpu.SMEM)
HBM = pl.BlockSpec(memory_space=pltpu.HBM)


def call(kernel, out_shape, args, in_specs=None, scratch=(), room=8, flops=0, **more):
    shapes = [a if isinstance(a, jax.ShapeDtypeStruct) else jax.ShapeDtypeStruct(a, F32) for a in out_shape]
    moved = sum(a.size * a.dtype.itemsize for a in (*args, *shapes))
    return pl.pallas_call(
        kernel,
        in_specs=in_specs or [VMEM] * len(args),
        out_specs=more.pop("out_specs", [VMEM] * len(shapes)),
        out_shape=shapes,
        scratch_shapes=list(scratch),
        compiler_params=pltpu.CompilerParams(vmem_limit_bytes=room << 20),
        cost_estimate=pl.CostEstimate(flops=flops, bytes_accessed=moved, transcendentals=0),
        **more,
    )(*args)


def opened(coords, w_first, b_first, n):
    a, b = column(w_first[0:1, :], n), column(w_first[1:2, :], n)
    pre = a * coords[0:1, :] + b * coords[1:2, :] + column(b_first, n)
    return jnp.tanh(pre), a, b


def layer(weight, bias, hidden, slopes):
    n = hidden.shape[1]
    product = dot3(weight, join(stacked(hidden, slopes)))
    return jnp.tanh(product[:, :n] + column(bias, n)), product[:, n:]


def readout(w_last, hidden, slopes):
    row = jnp.broadcast_to(w_last, (SUB, w_last.shape[1]))
    return dot3(split(row), join(stacked(hidden, slopes)))


def edge_kernel(
    where, w_hbm, coords_hbm, first_hbm, b_first_hbm, b_hbm, last_hbm, fw_hbm, owner_hbm, face_hbm,
    hs, ps, th, tl, wh, wl, out, owners,
    w, coords, first, b_first, b, last, fw, owner, face, sem, small,
):
    layers, _, _ = w.shape
    n = coords.shape[1]
    pairs = (
        (coords_hbm, coords),
        (first_hbm, first),
        (b_first_hbm, b_first),
        (b_hbm, b),
        (last_hbm, last),
        (fw_hbm, fw),
        (owner_hbm, owner),
        (face_hbm, face),
    )
    copies = [pltpu.make_async_copy(src, dst, small.at[i]) for i, (src, dst) in enumerate(pairs)]
    for copy in copies:
        copy.start()
    for k in range(layers):
        pltpu.make_async_copy(w_hbm.at[k], w.at[k], sem.at[k]).start()
    for copy in copies:
        copy.wait()
    hidden, a, c = opened(coords[...], first[...], b_first[...], n)
    hs[0] = hidden
    ps[0, :, :n] = a
    ps[0, :, n:] = c

    def body(k, carry):
        pltpu.make_async_copy(w_hbm.at[k], w.at[k], sem.at[k]).wait()
        plain = w[k]
        high, low = split(plain)
        wh[k] = high
        wl[k] = low
        high, low = split(plain.T)
        th[k] = high
        tl[k] = low
        hidden, slopes = layer((high, low), b[pl.ds(k, 1), :], hs[k], ps[k])
        hs[k + 1] = hidden
        ps[k + 1] = slopes
        return carry

    lax.fori_loop(0, layers, body, 0)
    row = readout(last[...], hs[layers], ps[layers])[0:1, :]
    flux = fw[0:1, :] * row[:, n : 2 * n] + fw[1:2, :] * row[:, 2 * n :]
    hot = (owner[...] == lax.broadcasted_iota(jnp.int32, (out.shape[0], n), 0)).astype(F32)
    owners[...] = hot
    faces = (face[...] == lax.broadcasted_iota(jnp.int32, (FACE_DEV, n), 0)).astype(F32)
    out[...] = lax.dot_general(hot * flux, faces, NT, precision=exact, preferred_element_type=F32)


def edge_forward(me, wide, w_hidden, coords, w_first, b_first, b_hidden, w_last, flux_weight, owner, face):
    layers, d, _ = w_hidden.shape
    n = coords.shape[1]
    arrays = (w_hidden, coords, w_first, b_first, b_hidden, w_last, flux_weight, owner, face)
    arrays = tuple(pltpu.with_memory_space_constraint(a, pltpu.HBM) for a in arrays)
    args = (me, *arrays)
    half = jax.ShapeDtypeStruct(w_hidden.shape, BF16)
    return call(
        edge_kernel,
        [(layers + 1, d, n), (layers + 1, d, 2 * n), half, half, half, half, (wide, FACE_DEV), (wide, n)],
        args,
        in_specs=[SMEM] + [HBM] * len(arrays),
        scratch=[pltpu.VMEM(a.shape, a.dtype) for a in arrays]
        + [pltpu.SemaphoreType.DMA((layers,)), pltpu.SemaphoreType.DMA((len(arrays) - 1,))],
        room=ROOM["edge"],
        flops=18 * layers * d * d * n,
    )


def inner_kernel(k, first, last, *refs):
    refs = list(refs)
    take = lambda count: [refs.pop(0) for _ in range(count)]
    th, tl, b = take(3)
    if first:
        coords, w_first, b_first = take(3)
    else:
        h, p = take(2)
    if last:
        (w_last,) = take(1)
    if first:
        h0, p0 = take(2)
    h1, p1 = take(2)
    if first:
        n = coords.shape[1]
        hidden, a, c = opened(coords[...], w_first[...], b_first[...], n)
        h0[...] = hidden
        p0[:, :n] = a
        p0[:, n:] = c
        slopes = jnp.concatenate([a, c], 1)
    else:
        hidden, slopes = h[...], p[...]
    hidden, slopes = layer((th[k], tl[k]), b[k : k + 1, :], hidden, slopes)
    h1[...] = hidden
    p1[...] = slopes
    if last:
        (sums,) = take(1)
        sums[...] = readout(w_last[...], hidden, slopes)


def inner_forward(k, n, weights, b_hidden, start, w_last):
    _, d, _ = weights[0].shape
    first, last = len(start) == 3, w_last is not None
    args = (*weights, b_hidden, *start) + ((w_last,) if last else ())
    shapes = [(d, n), (d, 2 * n)] * (2 if first else 1) + ([(SUB, 3 * n)] if last else [])
    return call(
        functools.partial(inner_kernel, k, first, last),
        shapes,
        args,
        room=ROOM["inner"],
        flops=18 * d * d * n,
    )


def owner_of(me, own, other, position):
    a, b = own[position], other[position]
    if a == b:
        return me ^ a
    return me ^ jnp.where(me % 2 == 0, a, b)


def scatter(me, tables, per, flat, keep, send):
    count = len(tables[0])
    half = count // 2
    for position in range(count):
        target, place_at = (keep, position) if position < half else (send, position - half)
        first = owner_of(me, *tables, position) * SUB
        for unit in range(per):
            start = pl.multiple_of(first + unit * SUB * count, SUB)
            target[place_at, unit * SUB : (unit + 1) * SUB, :] = flat[pl.ds(start, SUB), :]


def differentials(hidden, slopes, cot):
    n = hidden.shape[1]
    scale = 1.0 - hidden * hidden
    d_hidden, d_0, d_1 = cot[:, :n], cot[:, n : 2 * n], cot[:, 2 * n :]
    d_scale = d_0 * slopes[:, :n] + d_1 * slopes[:, n:]
    return scale * (d_hidden - 2.0 * hidden * d_scale), scale * d_0, scale * d_1


def backward_kernel(k, opening, closing, tables, face_scale, inner_scale, per, narrow, *refs):
    refs = list(refs)
    take = lambda count: [refs.pop(0) for _ in range(count)]
    where, wh, wl = take(3)
    h_low, p_low, h_top, p_top, hs, ps = take(6)
    if opening:
        isums, velocity, source, full, owners, face, flux_weight, w_last = take(8)
    else:
        cot_in = take(2)
    if closing:
        coords = take(2)
        (g_last,) = take(1)
    keep, send = take(2)
    if not closing:
        cot_out = take(2)
    if opening:
        g_out, integral = take(2)
        cot_in = cot_out
    if closing:
        cot_out = cot_in
        keep_more, send_more = take(2)
    xh, xl, dh, dl, flat = take(5)
    if closing:
        cot_out = take(2)
    me = where[0]
    d = wh.shape[1]
    ni, ne = h_low.shape[1], hs.shape[2]
    sizes, offsets = (ni, ne), (0, 3 * ni)
    tops = ((h_top[...], p_top[...]), (hs[k + 1], ps[k + 1]))

    if opening:
        row = isums[0:1, :]
        res = velocity[0:1, :] * row[:, ni : 2 * ni] + velocity[1:2, :] * row[:, 2 * ni :]
        res = inner_scale * (res + row[:, :ni] - source[...])
        inner = (res, res * velocity[0:1, :], res * velocity[1:2, :])
        faces = (face[...] == lax.broadcasted_iota(jnp.int32, (FACE_DEV, ne), 0)).astype(F32)
        every = full[...]
        mine = lax.broadcasted_iota(jnp.int32, every.shape, 0) == me // narrow
        integral[...] = jnp.sum(jnp.where(mine, every, 0.0), 0, keepdims=True)
        found = lax.dot_general(every, faces, NN, precision=exact, preferred_element_type=F32)
        found = face_scale * jnp.sum(owners[...] * found, 0, keepdims=True)
        edge = (jnp.zeros_like(found), found * flux_weight[0:1, :], found * flux_weight[1:2, :])
        total = None
        lift = column(w_last[...], LANES)
        for group, rows in enumerate((inner, edge)):
            n = sizes[group]
            line = jnp.concatenate(rows, 1)
            for tile in range(3 * n // LANES):
                at = slice(tile * LANES, (tile + 1) * LANES)
                cot_in[group][:, at] = lift * line[:, at]
            x = join(stacked(*tops[group]))
            part = dot3(split(jnp.broadcast_to(line, (SUB, 3 * n))), x, NT)
            total = part if total is None else total + part
        g_out[...] = total

    for group in (0, 1):
        n, at = sizes[group], offsets[group]
        for j, part in enumerate(differentials(*tops[group], cot_in[group][...])):
            high, low = split(part)
            dh[:, at + j * n : at + (j + 1) * n] = high
            dl[:, at + j * n : at + (j + 1) * n] = low
        low_level = (h_low[...], p_low[...]) if group == 0 else (hs[k], ps[k])
        for j, (high, low) in enumerate(stacked(*low_level)):
            xh[:, at + j * n : at + (j + 1) * n] = high
            xl[:, at + j * n : at + (j + 1) * n] = low

    x, delta = (xh[...], xl[...]), (dh[...], dl[...])
    grad = dot3(x, delta, NT)
    for tile in range(d // LANES):
        flat[tile * d : (tile + 1) * d, :] = grad[:, tile * LANES : (tile + 1) * LANES]
    back = dot3((wh[k], wl[k]), delta)
    cot_out[0][...] = back[:, : 3 * ni]
    cot_out[1][...] = back[:, 3 * ni :]
    scatter(me, tables, per, flat, keep, send)

    if closing:
        total = None
        for group in (0, 1):
            n = sizes[group]
            low_level = (h_low[...], p_low[...]) if group == 0 else (hs[k], ps[k])
            delta = join([split(p) for p in differentials(*low_level, cot_out[group][...])])
            one, none = jnp.ones((1, n), F32), jnp.zeros((1, n), F32)
            c = coords[group]
            rows = jnp.concatenate(
                [
                    jnp.concatenate([c[0:1, :], one, none], 1),
                    jnp.concatenate([c[1:2, :], none, one], 1),
                    jnp.zeros((SUB - 2, 3 * n), F32),
                ],
                0,
            )
            part = dot3(split(rows), delta, NT)
            total = part if total is None else total + part
        line = lambda row: [row[:, t * LANES : (t + 1) * LANES] for t in range(d // LANES)]
        rows = line(g_last[0:1, :]) + line(total[0:1, :]) + line(total[1:2, :])
        while len(rows) % SUB:
            rows.append(jnp.zeros((1, LANES), F32))
        pages = [jnp.concatenate(rows[i : i + SUB], 0) for i in range(0, len(rows), SUB)]
        half = len(tables[0]) // 2
        for position in range(2 * half):
            owner = owner_of(me, *tables, position)
            value = jnp.zeros((SUB, LANES), F32)
            for i, page in enumerate(pages):
                value = jnp.where(owner == i, page, value)
            if position < half:
                keep_more[position] = value
            else:
                send_more[position - half] = value


def backward(k, me, weights, low, top, edge, opened, carried, closed, tables, scales, narrow):
    opening, closing = opened is not None, closed is not None
    d = weights[0].shape[1]
    ni, ne = low[0].shape[1], edge[0].shape[2]
    count = len(tables[0])
    half = count // 2
    per = d * d // LANES // (SUB * count)
    args = (me, *weights, *low, *top, *edge, *(opened if opening else carried), *(closed or ()))
    shapes = [(half, per * SUB, LANES)] * 2
    if not closing:
        shapes += [(d, 3 * ni), (d, 3 * ne)]
    if opening:
        shapes += [(SUB, d), (1, FACE_DEV)]
    if closing:
        shapes += [(half, SUB, LANES)] * 2
    scratch = [pltpu.VMEM((d, 3 * (ni + ne)), BF16)] * 4 + [pltpu.VMEM((d * d // LANES, LANES), F32)]
    if closing:
        scratch += [pltpu.VMEM((d, 3 * ni), F32), pltpu.VMEM((d, 3 * ne), F32)]
    return call(
        functools.partial(backward_kernel, k, opening, closing, tables, *scales, per, narrow),
        shapes,
        args,
        in_specs=[SMEM] + [VMEM] * (len(args) - 1),
        scratch=scratch,
        room=ROOM["backward"],
        flops=36 * d * d * (ni + ne),
    )


def hop(array, pairs):
    return lax.ppermute(array, AXES, pairs)


def orders_of(count, even, odd):
    bits = [1 << i for i in range(1, count.bit_length() - 1)]

    def turned(by):
        by = by % max(1, len(bits) - 1)
        return bits[by:-1] + bits[:by] + bits[-1:]

    return turned(even), turned(odd)


def tables_of(orders):
    def offsets(order):
        found = [0]
        for bit in reversed(order):
            found = found + [bit ^ f for f in found]
        return found

    even, odd = offsets(orders[0]), offsets(orders[1])
    return tuple(even + [1 ^ f for f in odd]), tuple(odd + [1 ^ f for f in even])


def pairs_of(count, orders, stage):
    if stage == 0:
        return [(i, i ^ 1) for i in range(count)]
    return [(i, i ^ orders[i % 2][stage - 1]) for i in range(count)]


def total(count, orders, held):
    stages = count.bit_length() - 1
    for stage in range(1, stages - 1):
        middle = held.shape[0] // 2
        held = held[:middle] + hop(held[middle:], pairs_of(count, orders, stage))
    came = hop(held, pairs_of(count, orders, stages - 1))
    held = held + jnp.concatenate([came[1:], came[:1]], 0)
    for stage in range(stages - 2, 0, -1):
        held = jnp.concatenate([held, hop(held, pairs_of(count, orders, stage))], 0)
    return held, hop(held, pairs_of(count, orders, 0))


def gather_kernel(layers, tables, per, small, aliased, *refs):
    refs = list(refs)
    take = lambda count: [refs.pop(0) for _ in range(count)]
    where, *halves = take(3)
    if aliased:
        take(1)
    (out,) = take(1)
    g_first, g_last = take(2) if small else (None, None)
    buffer, sem = take(2)
    me = where[0]
    count = len(tables[0])
    d = buffer.shape[1]
    rows = SUB * count
    owners = [owner_of(me, *tables, position) for position in range(count)]
    for index, level in enumerate(layers):
        for position in range(count):
            source = halves[position // (count // 2)]
            first = owners[position] * SUB
            for unit in range(per):
                at = (index * per + unit) * SUB
                value = source[position % (count // 2), at : at + SUB, :]
                if rows <= d:
                    tile = unit * rows // d
                    start = pl.multiple_of(first + unit * rows % d, SUB)
                    buffer[index, pl.ds(start, SUB), tile * LANES : (tile + 1) * LANES] = value
                else:
                    flat = first + unit * rows
                    start = pl.multiple_of(flat % d, SUB)
                    tile = pl.multiple_of(flat // d * LANES, LANES)
                    buffer[index, pl.ds(start, SUB), pl.ds(tile, LANES)] = value
        pltpu.make_async_copy(buffer.at[index], out.at[level], sem.at[index]).start()
    if small:
        pages = [jnp.zeros((SUB, LANES), F32)] * -(-3 * d // (SUB * LANES))
        at = len(layers) * per * SUB
        for position in range(count):
            value = halves[position // (count // 2)][position % (count // 2), at : at + SUB, :]
            pages = [jnp.where(owners[position] == i, value, page) for i, page in enumerate(pages)]
        tiles = d // LANES
        for i in range(3 * tiles):
            row = pages[i // SUB][i % SUB : i % SUB + 1, :]
            lanes = slice(i % tiles * LANES, (i % tiles + 1) * LANES)
            if i < tiles:
                g_last[:, lanes] = row
            else:
                g_first[i // tiles - 1 : i // tiles, lanes] = row
    for index, level in enumerate(layers):
        pltpu.make_async_copy(buffer.at[index], out.at[level], sem.at[index]).wait()


def gather(me, shape, layers, tables, parts, before, small):
    _, d, _ = shape
    count = len(tables[0])
    per = d * d // LANES // (SUB * count)
    aliased = before is not None
    args = (me, *parts) + ((before,) if aliased else ())
    return call(
        functools.partial(gather_kernel, layers, tables, per, small, aliased),
        [shape] + ([(2, d), (1, d)] if small else []),
        args,
        in_specs=[SMEM, VMEM, VMEM] + ([HBM] if aliased else []),
        out_specs=[HBM] + ([VMEM, VMEM] if small else []),
        scratch=[pltpu.VMEM((len(layers), d, d), F32), pltpu.SemaphoreType.DMA((len(layers),))],
        room=ROOM["gather"],
        input_output_aliases={3: 0} if aliased else {},
    )


def local(
    coords_inner,
    velocity,
    source,
    coords_edge,
    flux_weight,
    owner,
    local_face,
    w_first,
    b_first,
    w_hidden,
    b_hidden,
    w_last,
):
    wide, narrow = lax.axis_size("wide"), lax.axis_size("narrow")
    count = wide * narrow
    layers, d = w_hidden.shape[:2]
    ni, ne = coords_inner.shape[1], coords_edge.shape[1]
    inner_scale = 2.0 / math.sqrt(ni * count)
    face_scale = 2.0 * penalty_weight / math.sqrt(FACE_DEV * wide)
    index = lax.axis_index("wide") * narrow + lax.axis_index("narrow")
    me = index.astype(jnp.int32)[None]
    face, owner = local_face[None], owner.reshape(1, ne)
    b_first, w_last, source = b_first[None], w_last[None], source[None]

    hs, ps, th, tl, wh, wl, full, owners = edge_forward(
        me, wide, w_hidden, coords_edge, w_first, b_first, b_hidden, w_last, flux_weight, owner, face
    )
    for bit in range(count.bit_length() - 1):
        full = full + hop(full, [(i, i ^ (1 << bit)) for i in range(count)])
    levels = []
    start = (coords_inner, w_first, b_first)
    for k in range(layers):
        found = inner_forward(k, ni, (th, tl), b_hidden, start, w_last if k == layers - 1 else None)
        if k == 0:
            levels.append(tuple(found[:2]))
            found = found[2:]
        start = tuple(found[:2])
        levels.append(start)
    isums = found[2]

    chunks = CHUNKS(layers)
    carried = None
    grad = None
    summed = []
    for layers_of, turns in chunks:
        orders = orders_of(count, *turns)
        tables = tables_of(orders)
        held = []
        for k in layers_of:
            opened = (isums, velocity, source, full, owners, face, flux_weight, w_last) if k == layers - 1 else None
            closed = (coords_inner, coords_edge, g_last) if k == 0 else None
            keep, send, *rest = backward(
                k, me, (wh, wl), levels[k], levels[k + 1], (hs, ps), opened, carried, closed, tables,
                (face_scale, inner_scale), narrow,
            )
            if opened:
                g_last, integral = rest[2:]
            if closed:
                keep, send = jnp.concatenate([keep, rest[0]], 1), jnp.concatenate([send, rest[1]], 1)
            else:
                carried = tuple(rest[:2])
            held.append(keep + hop(send, pairs_of(count, orders, 0)))
        held = held[0] if len(held) == 1 else jnp.concatenate(held, 1)
        summed.append((layers_of, tables, total(count, orders, held)))
    for layers_of, tables, parts in summed:
        found = gather(me, (layers, d, d), layers_of, tables, parts, grad, 0 in layers_of)
        grad = found[0]
        if 0 in layers_of:
            g_first, g_last = found[1:]
    return (integral.reshape(-1), g_first, grad, g_last.reshape(-1))


def solution(mesh):
    placed = (
        P(None, AXES),
        P(None, AXES),
        P(AXES),
        P(None, AXES),
        P(None, AXES),
        P(AXES, None),
        P(AXES),
        P(),
        P(),
        P(),
        P(),
        P(),
    )

    return jax.shard_map(
        local, mesh=mesh, in_specs=placed, out_specs=(P("wide"), P(), P(), P()), check_vma=False
    )
```

```python
import functools
import math

import jax
import jax.numpy as jnp
from jax import lax
from jax.experimental import pallas as pl
from jax.experimental.pallas import tpu as pltpu
from jax.sharding import PartitionSpec as P


FACE_DEV = 128
LANES = 128
SUB = 8
AXES = ("wide", "narrow")
ROOM = {"edge": 8, "inner": 3, "backward": 11, "gather": 4}


def CHUNKS():
    return (((3, 2), (0, 1)), ((1,), (2, 0)), ((0,), (0, 1)))


F32, BF16 = jnp.float32, jnp.bfloat16
exact = lax.Precision.HIGHEST
penalty_weight = 4.0
NN = (((1,), (0,)), ((), ()))
NT = (((1,), (1,)), ((), ()))


def split(x):
    high = x.astype(BF16)
    return high, (x - high.astype(F32)).astype(BF16)


def dot(a, b, dims=NN):
    return lax.dot_general(a, b, dims, preferred_element_type=F32)


def dot3(a, b, dims=NN):
    return dot(a[0], b[0], dims) + (dot(a[0], b[1], dims) + dot(a[1], b[0], dims))


def column(row, count):
    turned = jnp.broadcast_to(row, (LANES, row.shape[1])).T
    return jnp.concatenate([turned] * (count // LANES), 1)


def stacked(hidden, slopes):
    n = hidden.shape[1]
    scale = 1.0 - hidden * hidden
    return split(hidden), split(scale * slopes[:, :n]), split(scale * slopes[:, n:])


VMEM = pl.BlockSpec(memory_space=pltpu.VMEM)
SMEM = pl.BlockSpec(memory_space=pltpu.SMEM)
HBM = pl.BlockSpec(memory_space=pltpu.HBM)


def call(kernel, out_shape, args, in_specs=None, scratch=(), room=8, flops=0, **more):
    shapes = [a if isinstance(a, jax.ShapeDtypeStruct) else jax.ShapeDtypeStruct(a, F32) for a in out_shape]
    moved = sum(a.size * a.dtype.itemsize for a in (*args, *shapes))
    return pl.pallas_call(
        kernel,
        in_specs=in_specs or [VMEM] * len(args),
        out_specs=more.pop("out_specs", [VMEM] * len(shapes)),
        out_shape=shapes,
        scratch_shapes=list(scratch),
        compiler_params=pltpu.CompilerParams(vmem_limit_bytes=room << 20),
        cost_estimate=pl.CostEstimate(flops=flops, bytes_accessed=moved, transcendentals=0),
        **more,
    )(*args)


def opened(coords, w_first, b_first, n):
    a, b = column(w_first[0:1, :], n), column(w_first[1:2, :], n)
    pre = a * coords[0:1, :] + b * coords[1:2, :] + column(b_first, n)
    return jnp.tanh(pre), a, b


def keep_inputs(hidden, slopes, high, low):
    n = hidden.shape[1]
    for j, (h, l) in enumerate(stacked(hidden, slopes)):
        high[:, j * n : (j + 1) * n] = h
        low[:, j * n : (j + 1) * n] = l


def layer(weight, bias, x):
    product = dot3(weight, x)
    n = product.shape[1] // 3
    return jnp.tanh(product[:, :n] + column(bias, n)), product[:, n:]


def readout(w_last, hidden, slopes):
    n = hidden.shape[1]
    weight = column(w_last, n)
    scaled = weight * (1.0 - hidden * hidden)
    rows = (weight * hidden, scaled * slopes[:, :n], scaled * slopes[:, n:])
    return jnp.concatenate([jnp.sum(row, 0, keepdims=True) for row in rows], 1)


def folded(array):
    return sum(array[:, at : at + LANES] for at in range(LANES, array.shape[1], LANES)) + array[:, :LANES]


def row_sums(array):
    ones = jnp.ones((SUB, LANES), F32)
    return lax.dot_general(ones, array, NT, precision=exact, preferred_element_type=F32)[0:1, :]


def edge_kernel(
    where, w_hbm, coords_hbm, first_hbm, b_first_hbm, b_hbm, last_hbm, fw_hbm, owner_hbm, face_hbm,
    hs, ps, xh, xl, th, tl, wh, wl, out, owners,
    w, coords, first, b_first, b, last, fw, owner, face, sem, small,
):
    layers, _, _ = w.shape
    n = coords.shape[1]
    pairs = (
        (coords_hbm, coords),
        (first_hbm, first),
        (b_first_hbm, b_first),
        (b_hbm, b),
        (last_hbm, last),
        (fw_hbm, fw),
        (owner_hbm, owner),
        (face_hbm, face),
    )
    copies = [pltpu.make_async_copy(src, dst, small.at[i]) for i, (src, dst) in enumerate(pairs)]
    for copy in copies:
        copy.start()
    for k in range(layers):
        pltpu.make_async_copy(w_hbm.at[k], w.at[k], sem.at[k]).start()
    for copy in copies:
        copy.wait()
    hidden, a, c = opened(coords[...], first[...], b_first[...], n)
    hs[0] = hidden
    ps[0, :, :n] = a
    ps[0, :, n:] = c

    def prepare(k):
        pltpu.make_async_copy(w_hbm.at[k], w.at[k], sem.at[k]).wait()
        plain = w[k]
        high, low = split(plain)
        wh[k] = high
        wl[k] = low
        high, low = split(plain.T)
        th[k] = high
        tl[k] = low

    prepare(0)
    for k in range(layers):
        if k + 1 < layers:
            prepare(k + 1)
        keep_inputs(hs[k], ps[k], xh.at[k], xl.at[k])
        hidden, slopes = layer((th[k], tl[k]), b[k : k + 1, :], (xh[k], xl[k]))
        hs[k + 1] = hidden
        ps[k + 1] = slopes
    row = readout(last[...], hs[layers], ps[layers])
    flux = fw[0:1, :] * row[:, n : 2 * n] + fw[1:2, :] * row[:, 2 * n :]
    hot = (owner[...] == lax.broadcasted_iota(jnp.int32, (out.shape[0], n), 0)).astype(F32)
    owners[...] = hot
    faces = (face[...] == lax.broadcasted_iota(jnp.int32, (FACE_DEV, n), 0)).astype(F32)
    out[...] = lax.dot_general(hot * flux, faces, NT, precision=exact, preferred_element_type=F32)


def edge_forward(me, wide, w_hidden, coords, w_first, b_first, b_hidden, w_last, flux_weight, owner, face):
    layers, d, _ = w_hidden.shape
    n = coords.shape[1]
    arrays = (w_hidden, coords, w_first, b_first, b_hidden, w_last, flux_weight, owner, face)
    arrays = tuple(pltpu.with_memory_space_constraint(a, pltpu.HBM) for a in arrays)
    args = (me, *arrays)
    half = jax.ShapeDtypeStruct(w_hidden.shape, BF16)
    return call(
        edge_kernel,
        [
            *((layers + 1, d, n), (layers + 1, d, 2 * n)),
            *[jax.ShapeDtypeStruct((layers, d, 3 * n), BF16)] * 2,
            *[half] * 4,
            *((wide, FACE_DEV), (wide, n)),
        ],
        args,
        in_specs=[SMEM] + [HBM] * len(arrays),
        scratch=[pltpu.VMEM(a.shape, a.dtype) for a in arrays]
        + [pltpu.SemaphoreType.DMA((layers,)), pltpu.SemaphoreType.DMA((len(arrays) - 1,))],
        room=ROOM["edge"],
        flops=18 * layers * d * d * n,
    )


def inner_kernel(k, first, last, *refs):
    refs = list(refs)
    take = lambda count: [refs.pop(0) for _ in range(count)]
    th, tl, b = take(3)
    if first:
        coords, w_first, b_first = take(3)
    else:
        h, p = take(2)
    if last:
        (w_last,) = take(1)
    if first:
        h0, p0 = take(2)
    h1, p1, xh, xl = take(4)
    if first:
        n = coords.shape[1]
        hidden, a, c = opened(coords[...], w_first[...], b_first[...], n)
        h0[...] = hidden
        p0[:, :n] = a
        p0[:, n:] = c
        slopes = jnp.concatenate([a, c], 1)
    else:
        hidden, slopes = h[...], p[...]
    keep_inputs(hidden, slopes, xh, xl)
    hidden, slopes = layer((th[k], tl[k]), b[k : k + 1, :], (xh[...], xl[...]))
    h1[...] = hidden
    p1[...] = slopes
    if last:
        (sums,) = take(1)
        sums[...] = readout(w_last[...], hidden, slopes)


def inner_forward(k, n, weights, b_hidden, start, w_last):
    _, d, _ = weights[0].shape
    first, last = len(start) == 3, w_last is not None
    args = (*weights, b_hidden, *start) + ((w_last,) if last else ())
    shapes = [(d, n), (d, 2 * n)] * (2 if first else 1)
    shapes += [jax.ShapeDtypeStruct((d, 3 * n), BF16)] * 2 + ([(1, 3 * n)] if last else [])
    return call(
        functools.partial(inner_kernel, k, first, last),
        shapes,
        args,
        room=ROOM["inner"],
        flops=18 * d * d * n,
    )


def owner_of(me, own, other, position):
    a, b = own[position], other[position]
    if a == b:
        return me ^ a
    return me ^ jnp.where(me % 2 == 0, a, b)


def scatter(me, tables, per, flat, keep, send):
    count = len(tables[0])
    half = count // 2
    for position in range(count):
        target, place_at = (keep, position) if position < half else (send, position - half)
        first = owner_of(me, *tables, position) * SUB
        for unit in range(per):
            start = pl.multiple_of(first + unit * SUB * count, SUB)
            target[place_at, unit * SUB : (unit + 1) * SUB, :] = flat[pl.ds(start, SUB), :]


def differentials(hidden, slopes, cot):
    n = hidden.shape[1]
    scale = 1.0 - hidden * hidden
    d_hidden, d_0, d_1 = cot[:, :n], cot[:, n : 2 * n], cot[:, 2 * n :]
    d_scale = d_0 * slopes[:, :n] + d_1 * slopes[:, n:]
    return scale * (d_hidden - 2.0 * hidden * d_scale), scale * d_0, scale * d_1


def backward_kernel(k, opening, closing, tables, face_scale, inner_scale, per, narrow, *refs):
    refs = list(refs)
    take = lambda count: [refs.pop(0) for _ in range(count)]
    where, wh, wl = take(3)
    xh, xl, h_top, p_top, hs, ps, eh, el = take(8)
    if opening:
        isums, velocity, source, full, owners, face, flux_weight, w_last = take(8)
    else:
        cot_in = take(2)
    if closing:
        low = take(2)
        coords = take(2)
        (g_last,) = take(1)
    keep, send = take(2)
    if not closing:
        cot_out = take(2)
    if opening:
        g_out, integral = take(2)
        cot_in = cot_out
    if closing:
        keep_more, send_more = take(2)
    deltas = (take(2), take(2))
    (flat,) = take(1)
    if closing:
        cot_out = take(2)
    me = where[0]
    d = wh.shape[1]
    tops = ((h_top[...], p_top[...]), (hs[k + 1], ps[k + 1]))
    sizes = tuple(top[0].shape[1] for top in tops)
    ni, ne = sizes

    if opening:
        row = isums[...]
        res = velocity[0:1, :] * row[:, ni : 2 * ni] + velocity[1:2, :] * row[:, 2 * ni :]
        res = inner_scale * (res + row[:, :ni] - source[...])
        inner = (res, res * velocity[0:1, :], res * velocity[1:2, :])
        faces = (face[...] == lax.broadcasted_iota(jnp.int32, (FACE_DEV, ne), 0)).astype(F32)
        every = full[...]
        mine = lax.broadcasted_iota(jnp.int32, every.shape, 0) == me // narrow
        integral[...] = jnp.sum(jnp.where(mine, every, 0.0), 0, keepdims=True)
        found = lax.dot_general(every, faces, NN, precision=exact, preferred_element_type=F32)
        found = face_scale * jnp.sum(owners[...] * found, 0, keepdims=True)
        edge = (jnp.zeros_like(found), found * flux_weight[0:1, :], found * flux_weight[1:2, :])
        total = None
        lift = column(w_last[...], LANES)
        for group, rows in enumerate((inner, edge)):
            n = sizes[group]
            line = jnp.concatenate(rows, 1)
            for tile in range(3 * n // LANES):
                at = slice(tile * LANES, (tile + 1) * LANES)
                cot_in[group][:, at] = lift * line[:, at]
            hidden, slopes = tops[group]
            scale = 1.0 - hidden * hidden
            terms = hidden * rows[0] + scale * (slopes[:, :n] * rows[1] + slopes[:, n:] * rows[2])
            part = folded(terms)
            total = part if total is None else total + part
        g_out[...] = jnp.broadcast_to(row_sums(total), g_out.shape)

    for group in (0, 1):
        n = sizes[group]
        for j, part in enumerate(differentials(*tops[group], cot_in[group][...])):
            high, low_part = split(part)
            deltas[group][0][:, j * n : (j + 1) * n] = high
            deltas[group][1][:, j * n : (j + 1) * n] = low_part

    values = [(pair[0][...], pair[1][...]) for pair in deltas]
    grad = dot3((xh[...], xl[...]), values[0], NT) + dot3((eh[k], el[k]), values[1], NT)
    for tile in range(d // LANES):
        flat[tile * d : (tile + 1) * d, :] = grad[:, tile * LANES : (tile + 1) * LANES]
    for group in (0, 1):
        cot_out[group][...] = dot3((wh[k], wl[k]), values[group])
    scatter(me, tables, per, flat, keep, send)

    if closing:
        sums = [None, None]
        for group in (0, 1):
            level = (low[0][...], low[1][...]) if group == 0 else (hs[k], ps[k])
            d_pre, *d_slopes = differentials(*level, cot_out[group][...])
            for j in (0, 1):
                part = folded(d_pre * coords[group][j : j + 1, :] + d_slopes[j])
                sums[j] = part if sums[j] is None else sums[j] + part
        total = [row_sums(part) for part in sums]
        line = lambda row: [row[:, t * LANES : (t + 1) * LANES] for t in range(d // LANES)]
        rows = line(g_last[0:1, :]) + line(total[0]) + line(total[1])
        while len(rows) % SUB:
            rows.append(jnp.zeros((1, LANES), F32))
        pages = [jnp.concatenate(rows[i : i + SUB], 0) for i in range(0, len(rows), SUB)]
        half = len(tables[0]) // 2
        for position in range(2 * half):
            owner = owner_of(me, *tables, position)
            value = jnp.zeros((SUB, LANES), F32)
            for i, page in enumerate(pages):
                value = jnp.where(owner == i, page, value)
            if position < half:
                keep_more[position] = value
            else:
                send_more[position - half] = value


def backward(k, me, weights, inputs, top, edge, opened, carried, closed, tables, scales, narrow):
    opening, closing = opened is not None, closed is not None
    d = weights[0].shape[1]
    ni, ne = top[0].shape[1], edge[0].shape[2]
    count = len(tables[0])
    half = count // 2
    per = d * d // LANES // (SUB * count)
    args = (me, *weights, *inputs, *top, *edge, *(opened if opening else carried), *(closed or ()))
    shapes = [(half, per * SUB, LANES)] * 2
    if not closing:
        shapes += [(d, 3 * ni), (d, 3 * ne)]
    if opening:
        shapes += [(SUB, d), (1, FACE_DEV)]
    if closing:
        shapes += [(half, SUB, LANES)] * 2
    scratch = [pltpu.VMEM((d, 3 * n), BF16) for n in (ni, ni, ne, ne)]
    scratch += [pltpu.VMEM((d * d // LANES, LANES), F32)]
    if closing:
        scratch += [pltpu.VMEM((d, 3 * ni), F32), pltpu.VMEM((d, 3 * ne), F32)]
    return call(
        functools.partial(backward_kernel, k, opening, closing, tables, *scales, per, narrow),
        shapes,
        args,
        in_specs=[SMEM] + [VMEM] * (len(args) - 1),
        scratch=scratch,
        room=ROOM["backward"],
        flops=36 * d * d * (ni + ne),
    )


def hop(array, pairs):
    return lax.ppermute(array, AXES, pairs)


def orders_of(count, even, odd):
    bits = [1 << i for i in range(1, count.bit_length() - 1)]

    def turned(by):
        by = by % max(1, len(bits) - 1)
        return bits[by:-1] + bits[:by] + bits[-1:]

    return turned(even), turned(odd)


def tables_of(orders):
    def offsets(order):
        found = [0]
        for bit in reversed(order):
            found = found + [bit ^ f for f in found]
        return found

    even, odd = offsets(orders[0]), offsets(orders[1])
    return tuple(even + [1 ^ f for f in odd]), tuple(odd + [1 ^ f for f in even])


def pairs_of(count, orders, stage):
    if stage == 0:
        return [(i, i ^ 1) for i in range(count)]
    return [(i, i ^ orders[i % 2][stage - 1]) for i in range(count)]


def total(count, orders, held):
    stages = count.bit_length() - 1
    for stage in range(1, stages - 1):
        middle = held.shape[0] // 2
        held = held[:middle] + hop(held[middle:], pairs_of(count, orders, stage))
    came = hop(held, pairs_of(count, orders, stages - 1))
    held = held + jnp.concatenate([came[1:], came[:1]], 0)
    for stage in range(stages - 2, 0, -1):
        held = jnp.concatenate([held, hop(held, pairs_of(count, orders, stage))], 0)
    return held, hop(held, pairs_of(count, orders, 0))


def gather_kernel(layers, tables, per, small, aliased, *refs):
    refs = list(refs)
    take = lambda count: [refs.pop(0) for _ in range(count)]
    where, *halves = take(3)
    if aliased:
        take(1)
    (out,) = take(1)
    g_first, g_last = take(2) if small else (None, None)
    buffer, sem = take(2)
    me = where[0]
    count = len(tables[0])
    d = buffer.shape[1]
    rows = SUB * count
    owners = [owner_of(me, *tables, position) for position in range(count)]
    for index, level in enumerate(layers):
        for position in range(count):
            source = halves[position // (count // 2)]
            first = owners[position] * SUB
            for unit in range(per):
                at = (index * per + unit) * SUB
                value = source[position % (count // 2), at : at + SUB, :]
                if rows <= d:
                    tile = unit * rows // d
                    start = pl.multiple_of(first + unit * rows % d, SUB)
                    buffer[index, pl.ds(start, SUB), tile * LANES : (tile + 1) * LANES] = value
                else:
                    flat = first + unit * rows
                    start = pl.multiple_of(flat % d, SUB)
                    tile = pl.multiple_of(flat // d * LANES, LANES)
                    buffer[index, pl.ds(start, SUB), pl.ds(tile, LANES)] = value
        pltpu.make_async_copy(buffer.at[index], out.at[level], sem.at[index]).start()
    if small:
        pages = [jnp.zeros((SUB, LANES), F32)] * -(-3 * d // (SUB * LANES))
        at = len(layers) * per * SUB
        for position in range(count):
            value = halves[position // (count // 2)][position % (count // 2), at : at + SUB, :]
            pages = [jnp.where(owners[position] == i, value, page) for i, page in enumerate(pages)]
        tiles = d // LANES
        for i in range(3 * tiles):
            row = pages[i // SUB][i % SUB : i % SUB + 1, :]
            lanes = slice(i % tiles * LANES, (i % tiles + 1) * LANES)
            if i < tiles:
                g_last[:, lanes] = row
            else:
                g_first[i // tiles - 1 : i // tiles, lanes] = row
    for index, level in enumerate(layers):
        pltpu.make_async_copy(buffer.at[index], out.at[level], sem.at[index]).wait()


def gather(me, shape, layers, tables, parts, before, small):
    _, d, _ = shape
    count = len(tables[0])
    per = d * d // LANES // (SUB * count)
    aliased = before is not None
    args = (me, *parts) + ((before,) if aliased else ())
    return call(
        functools.partial(gather_kernel, layers, tables, per, small, aliased),
        [shape] + ([(2, d), (1, d)] if small else []),
        args,
        in_specs=[SMEM, VMEM, VMEM] + ([HBM] if aliased else []),
        out_specs=[HBM] + ([VMEM, VMEM] if small else []),
        scratch=[pltpu.VMEM((len(layers), d, d), F32), pltpu.SemaphoreType.DMA((len(layers),))],
        room=ROOM["gather"],
        input_output_aliases={3: 0} if aliased else {},
    )


def local(
    coords_inner,
    velocity,
    source,
    coords_edge,
    flux_weight,
    owner,
    local_face,
    w_first,
    b_first,
    w_hidden,
    b_hidden,
    w_last,
):
    wide, narrow = lax.axis_size("wide"), lax.axis_size("narrow")
    count = wide * narrow
    layers, d = w_hidden.shape[:2]
    ni, ne = coords_inner.shape[1], coords_edge.shape[1]
    inner_scale = 2.0 / math.sqrt(ni * count)
    face_scale = 2.0 * penalty_weight / math.sqrt(FACE_DEV * wide)
    index = lax.axis_index("wide") * narrow + lax.axis_index("narrow")
    me = index.astype(jnp.int32)[None]
    face, owner = local_face[None], owner.reshape(1, ne)
    b_first, w_last, source = b_first[None], w_last[None], source[None]

    hs, ps, eh, el, th, tl, wh, wl, full, owners = edge_forward(
        me, wide, w_hidden, coords_edge, w_first, b_first, b_hidden, w_last, flux_weight, owner, face
    )
    for bit in range(count.bit_length() - 1):
        full = full + hop(full, [(i, i ^ (1 << bit)) for i in range(count)])
    levels, inputs = [], []
    start = (coords_inner, w_first, b_first)
    for k in range(layers):
        found = inner_forward(k, ni, (th, tl), b_hidden, start, w_last if k == layers - 1 else None)
        if k == 0:
            levels.append(tuple(found[:2]))
            found = found[2:]
        start = tuple(found[:2])
        levels.append(start)
        inputs.append(tuple(found[2:4]))
    isums = found[4]

    chunks = CHUNKS()
    carried = None
    grad = None
    summed = []
    for layers_of, turns in chunks:
        orders = orders_of(count, *turns)
        tables = tables_of(orders)
        held = []
        for k in layers_of:
            opened = (isums, velocity, source, full, owners, face, flux_weight, w_last) if k == layers - 1 else None
            closed = (*levels[0], coords_inner, coords_edge, g_last) if k == 0 else None
            keep, send, *rest = backward(
                k, me, (wh, wl), inputs[k], levels[k + 1], (hs, ps, eh, el), opened, carried, closed, tables,
                (face_scale, inner_scale), narrow,
            )
            if opened:
                g_last, integral = rest[2:]
            if closed:
                keep, send = jnp.concatenate([keep, rest[0]], 1), jnp.concatenate([send, rest[1]], 1)
            else:
                carried = tuple(rest[:2])
            held.append(keep + hop(send, pairs_of(count, orders, 0)))
        held = held[0] if len(held) == 1 else jnp.concatenate(held, 1)
        summed.append((layers_of, tables, total(count, orders, held)))
    for layers_of, tables, parts in summed:
        found = gather(me, (layers, d, d), layers_of, tables, parts, grad, 0 in layers_of)
        grad = found[0]
        if 0 in layers_of:
            g_first, g_last = found[1:]
    return (integral.reshape(-1), g_first, grad, g_last.reshape(-1))


def solution(mesh):
    placed = (
        P(None, AXES),
        P(None, AXES),
        P(AXES),
        P(None, AXES),
        P(None, AXES),
        P(AXES, None),
        P(AXES),
        P(),
        P(),
        P(),
        P(),
        P(),
    )

    return jax.shard_map(
        local, mesh=mesh, in_specs=placed, out_specs=(P("wide"), P(), P(), P()), check_vma=False
    )
```
